32 devices in a mesh: region: 4 (over z), tracer: 2 (over x), sect: 4 (over y, core).
Axes of the slice: x: 2, y: 2, z: 4, core: 2. Of those that a mesh axis runs over, the one named last changes fastest.
Arguments:
- solute_concentration: float32 [16, 96, 32, 128], P('tracer', 'region', 'sect'), may hold values from 0.5 to 2
- thermal_anomaly: float32 [96, 32, 128], P('region', 'sect'), may hold values from -6 to 6
- eastward_flow_speed: float32 [96, 32, 128], P('region', 'sect'), may hold values from -1 to 1
- northward_flow_speed: float32 [96, 32, 128], P('region', 'sect'), may hold values from -1 to 1
- submerged_layers: int32 [96, 32], P('region', 'sect'), may hold values from 0 to 128, as said below
- interaction_matrix: float32 [16, 16], replicated, may hold values from -1.5 to 1.5
- bloom_yields: float32 [16], replicated, may hold values from -8 to 8
Outputs:
- tracers_next: float32 [16, 96, 32, 128], P('tracer', 'region', 'sect')
- temperature_next: float32 [96, 32, 128], P('region', 'sect')
The draws below stay inside these ranges and needn't reach their ends.
Inputs may be any that keep to these rules, and one draw needn't show every extreme that they name: `submerged_layers`: land (0) forms a few contiguous masses, with shallow shelves around them; columns far from land have all 128 levels.
All inputs are finite; a program needn't handle non-finite values.
Results may differ from the reference program's by a relative error of at most 0.0001.
Values sent between devices are 32-bit elements; how exact they have to be, the bound alone decides.
A program may use at most 64 MiB of HBM per device.

```python
import jax
import jax.numpy as jnp
from jax import lax

NTR = 16
DEPTH_LAYERS = 128
STEPS = 3
SUB = 4
GRID_EXTENT_EAST = 96
GRID_EXTENT_NORTH = 32


def draw_submerged_layers(key, part):
    keys = jax.random.split(jax.random.fold_in(key, 7), 4)
    count = 6
    centre_x = jax.random.randint(keys[0], (count,), 0, GRID_EXTENT_EAST)
    centre_y = jax.random.randint(keys[1], (count,), 0, GRID_EXTENT_NORTH)
    radius = jax.random.randint(keys[2], (count,), 3, 10)
    places_x = jnp.arange(GRID_EXTENT_EAST, dtype=jnp.int32)[:, None, None]
    places_y = jnp.arange(GRID_EXTENT_NORTH, dtype=jnp.int32)[None, :, None]
    dist_x = jnp.abs(places_x - centre_x[None, None, :])
    dist_x = jnp.minimum(dist_x, GRID_EXTENT_EAST - dist_x)
    dist_y = jnp.abs(places_y - centre_y[None, None, :])
    dist_y = jnp.minimum(dist_y, GRID_EXTENT_NORTH - dist_y)
    unit_x = dist_x * 64 // GRID_EXTENT_EAST
    unit_y = dist_y * 64 // GRID_EXTENT_NORTH
    excess = unit_x * unit_x + unit_y * unit_y - radius[None, None, :] * radius[None, None, :]
    nearest = jnp.min(excess, axis=2)
    jitter = jax.random.randint(keys[3], (GRID_EXTENT_EAST, GRID_EXTENT_NORTH), 0, DEPTH_LAYERS // 8 + 1)
    depth = jnp.minimum(DEPTH_LAYERS, DEPTH_LAYERS * jnp.maximum(nearest, 0) // 32 + 1 + jitter)
    return jnp.where(nearest < 0, 0, depth).astype(jnp.int32)


def block_levels(own_key, extent, cuts, smallest, largest):
    gain, own = 1.0, jax.random.fold_in(own_key, 6)
    for axis_at, parts in cuts:
        draws = jnp.exp(jax.random.uniform(jax.random.fold_in(own, axis_at), (parts,), jnp.float32, smallest / len(cuts), largest / len(cuts)))
        gain = gain * jnp.repeat(draws, extent[axis_at] // parts).reshape([-1 if axis == axis_at else 1 for axis in range(len(extent))])
    return gain


def noise(own_key, dims, scale, most, cuts=(), kind=jnp.bfloat16):
    gain = block_levels(own_key, dims, cuts, -0.22, 0.18) if cuts else 1.0
    drawn = jax.random.normal(own_key, dims, jnp.float32) * scale * gain
    return jnp.minimum(jnp.maximum(drawn, -most), most).astype(kind)


def setup_inputs(seed: int = 0) -> dict:
    arg_keys = jax.random.split(jax.random.key(seed), 8)
    return {
        "solute_concentration": jnp.clip(0.5 + 1.5 * jax.random.uniform(arg_keys[0], (NTR, GRID_EXTENT_EAST, GRID_EXTENT_NORTH, DEPTH_LAYERS), jnp.float32) ** block_levels(arg_keys[0], (NTR, GRID_EXTENT_EAST, GRID_EXTENT_NORTH, DEPTH_LAYERS), ((0, 2), (1, 4), (2, 4)), -0.2, 0.2), 0.5, 2.0),
        "thermal_anomaly": noise(arg_keys[1], (GRID_EXTENT_EAST, GRID_EXTENT_NORTH, DEPTH_LAYERS), 1.0, 6.0, ((0, 4), (1, 4)), jnp.float32),
        "eastward_flow_speed": jnp.clip(jax.random.uniform(arg_keys[2], (GRID_EXTENT_EAST, GRID_EXTENT_NORTH, DEPTH_LAYERS), jnp.float32, -1.0, 1.0) * block_levels(arg_keys[2], (GRID_EXTENT_EAST, GRID_EXTENT_NORTH, DEPTH_LAYERS), ((0, 4), (1, 4)), -0.4, 0.0), -1.0, 1.0),
        "northward_flow_speed": jnp.clip(jax.random.uniform(arg_keys[3], (GRID_EXTENT_EAST, GRID_EXTENT_NORTH, DEPTH_LAYERS), jnp.float32, -1.0, 1.0) * block_levels(arg_keys[3], (GRID_EXTENT_EAST, GRID_EXTENT_NORTH, DEPTH_LAYERS), ((0, 4), (1, 4)), -0.4, 0.0), -1.0, 1.0),
        "submerged_layers": draw_submerged_layers(jax.random.fold_in(arg_keys[7], 71), 0),
        "interaction_matrix": noise(arg_keys[5], (NTR, NTR), NTR ** -0.5, 1.5, (), jnp.float32),
        "bloom_yields": noise(arg_keys[6], (NTR,), 2.0, 8.0, (), jnp.float32),
    }


TIME_STEP = 0.2
REACT_STEP = 0.1
GROWTH_MAX = 1.0
HALF_SAT = 0.5
WATER_ATT = 3.0
CHL_ATT = 2.0
HEAT_GAIN = 0.5


def upwind_global(field, east_flux, north_flux):
    flux_x = jnp.maximum(east_flux, 0.0) * field + jnp.minimum(east_flux, 0.0) * jnp.roll(field, -1, axis=-3)
    flux_y = jnp.maximum(north_flux, 0.0) * field + jnp.minimum(north_flux, 0.0) * jnp.roll(field, -1, axis=-2)
    return flux_x - jnp.roll(flux_x, 1, axis=-3) + flux_y - jnp.roll(flux_y, 1, axis=-2)


def light(chl_abs, upper_ones):
    layer_total = chl_abs.shape[-1]
    cells = chl_abs.reshape(-1, layer_total)
    above = jnp.dot(cells, upper_ones, precision=lax.Precision.HIGHEST, preferred_element_type=jnp.float32)
    above = above.reshape(chl_abs.shape)
    depth = jnp.arange(layer_total, dtype=jnp.float32) + 0.5
    return jnp.exp(-(WATER_ATT / layer_total * depth + CHL_ATT / layer_total * (above + 0.5 * chl_abs)))


def react(mixture, interaction_matrix, bloom_yields, upper_ones):
    for substep in range(SUB):
        chl_abs = jnp.abs(mixture[1])
        nutrient = mixture[0]
        rate = GROWTH_MAX * light(chl_abs, upper_ones) * nutrient / (jnp.abs(nutrient) + HALF_SAT)
        linear = jnp.einsum("ab,bxyk->axyk", interaction_matrix, mixture, precision=lax.Precision.HIGHEST)
        tendency = linear + bloom_yields[:, None, None, None] * (rate * mixture[2])[None]
        mixture = mixture + REACT_STEP * tendency
    chl_abs = jnp.abs(mixture[1])
    heating = HEAT_GAIN * chl_abs * light(chl_abs, upper_ones)
    return mixture, heating


def reference(solute_concentration, thermal_anomaly, eastward_flow_speed, northward_flow_speed, submerged_layers, interaction_matrix, bloom_yields):
    water_mask = (jnp.arange(DEPTH_LAYERS, dtype=jnp.int32)[None, None, :] < submerged_layers[:, :, None]).astype(jnp.float32)
    east_flux = eastward_flow_speed * water_mask * jnp.roll(water_mask, -1, axis=0)
    north_flux = northward_flow_speed * water_mask * jnp.roll(water_mask, -1, axis=1)
    upper_ones = (jnp.arange(DEPTH_LAYERS)[:, None] < jnp.arange(DEPTH_LAYERS)[None, :]).astype(jnp.float32)
    mixture = solute_concentration
    warming_tendency = thermal_anomaly
    for section_index in range(STEPS):
        mixture = water_mask * (mixture - TIME_STEP * upwind_global(mixture, east_flux, north_flux))
        warming_tendency = water_mask * (warming_tendency - TIME_STEP * upwind_global(warming_tendency, east_flux, north_flux))
        mixture, heating = react(mixture, interaction_matrix, bloom_yields, upper_ones)
        warming_tendency = warming_tendency + TIME_STEP * water_mask * heating
    return mixture, warming_tendency
```

```python
import functools

import jax
import jax.numpy as jnp
from jax import lax
from jax.experimental import pallas as pl
from jax.experimental.pallas import tpu as pltpu
from jax.sharding import PartitionSpec as P

STEPS = 3
SUB = 4

TIME_STEP = 0.2
REACT_STEP = 0.1
GROWTH_MAX = 1.0
HALF_SAT = 0.5
WATER_ATT = 3.0
CHL_ATT = 2.0
HEAT_GAIN = 0.5

MESH = pl.DeviceIdType.MESH
HIGHEST = lax.Precision.HIGHEST
EAST, WEST, NORTH, SOUTH = range(4)


def iota(shape, dim):
    return lax.broadcasted_iota(jnp.int32, shape, dim)


def exact_dot(a, b, dims=((1,), (0,))):
    return lax.dot_general(
        a, b, (dims, ((), ())), precision=HIGHEST, preferred_element_type=jnp.float32
    )


def halves(x):
    high = x.astype(jnp.bfloat16)
    return high, (x - high.astype(jnp.float32)).astype(jnp.bfloat16)


def half_dot(a, b):
    return jnp.dot(a, b, preferred_element_type=jnp.float32)


def dot3(a, b):
    return half_dot(a[0], b[0]) + half_dot(a[1], b[0]) + half_dot(a[0], b[1])


def tables(rates_ref, yields_ref, tracers, wide, Y):
    rows = tracers * Y
    spread = (iota((rows, tracers), 0) // Y == iota((rows, tracers), 1)).astype(jnp.float32)
    same = iota((rows, rows), 0) % Y == iota((rows, rows), 1) % Y
    full = exact_dot(exact_dot(spread, rates_ref[...]), spread, ((1,), (1,)))
    full = jnp.where(same, full, 0.0) * REACT_STEP
    diagonal = (iota((rows, rows), 0) == iota((rows, rows), 1)).astype(jnp.float32)
    one = diagonal + full
    two = exact_dot(one, one)
    three = exact_dot(two, one)
    four = exact_dot(two, two)
    source = [
        exact_dot(spread * yields_ref[...], jnp.ones((tracers, wide), jnp.float32)) * REACT_STEP
    ]
    for power in (one, two, three):
        source.append(exact_dot(power, source[0]))
    head = jnp.concatenate([power[: 3 * Y] for power in (one, two, three)], axis=0)
    shape = (rows, wide)
    lane = iota(shape, 1)
    inject = jnp.zeros(shape, jnp.float32)
    for sub in range(SUB):
        hit = jnp.logical_and(lane // Y == sub, lane % Y == iota(shape, 0) % Y)
        inject = inject + jnp.where(hit, source[SUB - 1 - sub], 0.0)
    return head, four, inject[:, : SUB * Y], [v[: 3 * Y] for v in source[: SUB - 1]]


def stack(flat, wide):
    return jnp.concatenate(
        [flat[:, i * wide : (i + 1) * wide] for i in range(flat.shape[1] // wide)], axis=0
    )


def unstack(tall, Y):
    return jnp.concatenate(
        [tall[i * Y : (i + 1) * Y] for i in range(tall.shape[0] // Y)], axis=1
    )


def kernel(
    regions, groups, sects,
    solute, heat_in, east_in, north_in, layers_in, rates_ref, yields_ref,
    tracers_out, heat_out,
    state, ysend, yrecv, coef, final,
    in_send, in_recv, halo_send, halo_recv, out_send, out_recv, local_sem,
):
    region, group, sect = (lax.axis_index(a) for a in ("region", "tracer", "sect"))
    own, wide, Y = solute.shape[0], solute.shape[2], layers_in.shape[1]
    tracers = own * groups
    block = heat_in.shape[0] // groups
    span = block // Y
    fields = tracers + 1
    every = fields + 3

    def place(reg, t):
        return t + (reg % 2) * (groups - 1 - 2 * t)

    part = place(region, group)
    last = groups - 1
    next_region = lax.rem(region + 1, regions)
    past_region = lax.rem(region + regions - 1, regions)
    east_region = jnp.where(part == last, next_region, region)
    west_region = jnp.where(part == 0, past_region, region)
    east_part = jnp.where(part == last, 0, part + 1)
    west_part = jnp.where(part == 0, last, part - 1)
    beside = {
        EAST: {"region": east_region, "tracer": place(east_region, east_part)},
        WEST: {"region": west_region, "tracer": place(west_region, west_part)},
        NORTH: {"sect": lax.rem(sect + 1, sects)},
        SOUTH: {"sect": lax.rem(sect + sects - 1, sects)},
    }
    peers = [lax.rem(group + d, groups) for d in range(1, groups)]

    def rows_of(t):
        return pl.ds(pl.multiple_of(place(region, t) * block, Y), block)

    mine = rows_of(group)
    slot = pl.ds(group * own, own)
    inner = pl.ds(Y, block)

    barrier = pltpu.get_barrier_semaphore()
    for peer in peers:
        pl.semaphore_signal(barrier, inc=1, device_id={"tracer": peer}, device_id_type=MESH)
    for side in range(4):
        pl.semaphore_signal(barrier, inc=1, device_id=beside[side], device_id_type=MESH)
    keep = pltpu.make_async_copy(
        solute.at[:, mine, :], state.at[0, slot, inner, :], local_sem.at[0]
    )
    keep.start()
    pl.semaphore_wait(barrier, groups - 1 + 4)

    arriving = []
    for d, peer in enumerate(peers):
        copy = pltpu.make_async_remote_copy(
            src_ref=solute.at[:, rows_of(peer), :],
            dst_ref=state.at[0, slot, inner, :],
            send_sem=in_send.at[d],
            recv_sem=in_recv.at[d],
            device_id={"tracer": peer},
            device_id_type=MESH,
        )
        copy.start()
        arriving.append(copy)

    total = layers_in.shape[0] * Y
    pick = (iota((total, layers_in.shape[0]), 0) // Y == iota((total, layers_in.shape[0]), 1))
    depth = half_dot(
        pick.astype(jnp.bfloat16), layers_in[...].astype(jnp.float32).astype(jnp.bfloat16)
    )
    depth = jnp.where(iota((total, Y), 0) % Y == iota((total, Y), 1), depth, 0.0)
    depth = half_dot(depth.astype(jnp.bfloat16), jnp.ones((Y, wide), jnp.bfloat16))
    coef[5] = (iota((total, wide), 1).astype(jnp.float32) < depth).astype(jnp.float32)
    state[0, tracers, inner, :] = heat_in[mine, :]
    state[0, fields, inner, :] = east_in[mine, :]
    state[0, fields + 1, inner, :] = north_in[mine, :]
    state[0, fields + 2, inner, :] = coef[5, mine, :]

    head, four, inject, source = tables(rates_ref, yields_ref, tracers, wide, Y)
    head, four, inject = halves(head), halves(four), halves(inject)
    upper = (iota((wide, wide), 0) < iota((wide, wide), 1)).astype(jnp.bfloat16)
    level = iota((block, wide), 1).astype(jnp.float32) + 0.5
    tile = (1, span)
    source = [jnp.tile(v, tile) for v in source]

    def light(chl_abs):
        high, low = halves(chl_abs)
        above = half_dot(high, upper) + half_dot(low, upper)
        return jnp.exp(
            -(WATER_ATT / wide * level + CHL_ATT / wide * (above + 0.5 * chl_abs))
        )

    def exchange(step, count):
        some = pl.ds(0, count)
        for f in range(count):
            ysend[step, 0, f] = state[step, f, pl.ds(Y, span, stride=Y), :]
            ysend[step, 1, f] = state[step, f, pl.ds(2 * Y - 1, span, stride=Y), :]
        plan = {
            EAST: (state.at[step, some, pl.ds(block, Y), :], state.at[step, some, pl.ds(0, Y), :]),
            WEST: (
                state.at[step, some, pl.ds(Y, Y), :],
                state.at[step, some, pl.ds(block + Y, Y), :],
            ),
            NORTH: (ysend.at[step, 1, some], yrecv.at[step, 1, some]),
            SOUTH: (ysend.at[step, 0, some], yrecv.at[step, 0, some]),
        }
        copies = []
        for side, (source_ref, target_ref) in plan.items():
            copy = pltpu.make_async_remote_copy(
                src_ref=source_ref,
                dst_ref=target_ref,
                send_sem=halo_send.at[step, side],
                recv_sem=halo_recv.at[step, side],
                device_id=beside[side],
                device_id_type=MESH,
            )
            copy.start()
            copies.append(copy)
        return copies

    def beside_y(step, value, x, first, count):
        at = (count, Y, wide)
        row = iota(at, 1)
        some = pl.ds(first, count)
        above = jnp.broadcast_to(yrecv[step, 0, some, pl.ds(x, 1), :], at)
        below = jnp.broadcast_to(yrecv[step, 1, some, pl.ds(x, 1), :], at)
        up = jnp.where(row == Y - 1, above, pltpu.roll(value, Y - 1, 1))
        down = jnp.where(row == 0, below, pltpu.roll(value, 1, 1))
        return up, down

    keep.wait()
    for copy in arriving:
        copy.wait()

    for step in range(STEPS):
        for copy in exchange(step, every if step == 0 else fields):
            copy.wait()
        columns, heats, wets = [], [], []
        for x in range(span):
            here = pl.ds((x + 1) * Y, Y)
            ahead = pl.ds((x + 2) * Y, Y)
            behind = pl.ds(x * Y, Y)
            cell = pl.ds(x * Y, Y)
            if step == 0:
                speed_wet = state[0, pl.ds(fields + 1, 2), here, :]
                up, down = beside_y(0, speed_wet, x, fields + 1, 2)
                wet = speed_wet[1]
                east = state[0, fields, here, :] * wet * state[0, fields + 2, ahead, :]
                west = state[0, fields, behind, :] * state[0, fields + 2, behind, :] * wet
                north = speed_wet[0] * wet * up[1]
                south = down[0] * down[1] * wet
                scaled = TIME_STEP * wet
                coef[0, cell, :] = wet - scaled * (
                    jnp.maximum(east, 0.0) - jnp.minimum(west, 0.0)
                    + jnp.maximum(north, 0.0) - jnp.minimum(south, 0.0)
                )
                coef[1, cell, :] = -scaled * jnp.minimum(east, 0.0)
                coef[2, cell, :] = scaled * jnp.maximum(west, 0.0)
                coef[3, cell, :] = -scaled * jnp.minimum(north, 0.0)
                coef[4, cell, :] = scaled * jnp.maximum(south, 0.0)
            value = state[step, pl.ds(0, fields), here, :]
            up, down = beside_y(step, value, x, 0, fields)
            moved = (
                coef[0, cell, :] * value
                + coef[1, cell, :] * state[step, pl.ds(0, fields), ahead, :]
                + coef[2, cell, :] * state[step, pl.ds(0, fields), behind, :]
                + coef[3, cell, :] * up
                + coef[4, cell, :] * down
            )
            columns.append(moved[:tracers].reshape(tracers * Y, wide))
            heats.append(moved[tracers])
            wets.append(state[0, fields + 2, here, :])
        mixed = jnp.concatenate(columns, axis=1)
        parts = halves(mixed)
        ahead_rows = dot3(head, parts)
        result = dot3(four, parts)
        rates = []
        for sub in range(SUB):
            if sub == 0:
                rows = mixed[: 3 * Y]
            else:
                rows = ahead_rows[(sub - 1) * 3 * Y : sub * 3 * Y]
                for i, rate in enumerate(rates):
                    rows = rows + source[sub - 1 - i] * jnp.concatenate([rate] * 3, axis=0)
            nutrient, chl, phyto = rows[:Y], rows[Y : 2 * Y], rows[2 * Y :]
            shade = unstack(light(jnp.abs(stack(chl, wide))), Y)
            rates.append(
                GROWTH_MAX * shade * nutrient / (jnp.abs(nutrient) + HALF_SAT) * phyto
            )
        result = result + dot3(inject, halves(jnp.concatenate(rates, axis=0)))
        chl_abs = jnp.abs(stack(result[Y : 2 * Y], wide))
        heating = HEAT_GAIN * chl_abs * light(chl_abs)
        heat = jnp.concatenate(heats, axis=0) + TIME_STEP * jnp.concatenate(wets, axis=0) * heating
        if step < STEPS - 1:
            target, base = state.at[step + 1], Y
        else:
            target, base = final, 0
        for x in range(span):
            target[pl.ds(0, tracers), pl.ds(base + x * Y, Y), :] = result[
                :, x * wide : (x + 1) * wide
            ].reshape(tracers, Y, wide)
        target[tracers, pl.ds(base, block), :] = heat

    leaving = []
    for d, peer in enumerate(peers):
        pairs = (
            (final.at[pl.ds(peer * own, own)], tracers_out.at[:, mine, :]),
            (final.at[tracers], heat_out.at[mine, :]),
        )
        for i, (source_ref, target_ref) in enumerate(pairs):
            copy = pltpu.make_async_remote_copy(
                src_ref=source_ref,
                dst_ref=target_ref,
                send_sem=out_send.at[d, i],
                recv_sem=out_recv.at[d, i],
                device_id={"tracer": peer},
                device_id_type=MESH,
            )
            copy.start()
            leaving.append(copy)
    for i, (source_ref, target_ref) in enumerate(
        ((final.at[slot], tracers_out.at[:, mine, :]), (final.at[tracers], heat_out.at[mine, :]))
    ):
        copy = pltpu.make_async_copy(source_ref, target_ref, local_sem.at[1 + i])
        copy.start()
        leaving.append(copy)
    for copy in leaving:
        copy.wait()


def solution(mesh):
    regions, groups, sects = (mesh.shape[a] for a in ("region", "tracer", "sect"))

    def body(solute, thermal, eastward, northward, layers, rates, yields):
        own, rows, cols, wide = solute.shape
        tracers = own * groups
        span = rows // groups
        fields = tracers + 1
        flat = (rows * cols, wide)
        vmem, hbm = pl.BlockSpec(memory_space=pltpu.VMEM), pl.BlockSpec(memory_space=pl.ANY)
        dma = pltpu.SemaphoreType.DMA
        peers = max(groups - 1, 1)
        mixture, heat = pl.pallas_call(
            functools.partial(kernel, regions, groups, sects),
            out_shape=(
                jax.ShapeDtypeStruct((own, *flat), jnp.float32),
                jax.ShapeDtypeStruct(flat, jnp.float32),
            ),
            in_specs=[hbm] + [vmem] * 6,
            out_specs=(hbm, hbm),
            scratch_shapes=[
                pltpu.VMEM((STEPS, fields + 3, (span + 2) * cols, wide), jnp.float32),
                pltpu.VMEM((STEPS, 2, fields + 3, span, wide), jnp.float32),
                pltpu.VMEM((STEPS, 2, fields + 3, span, wide), jnp.float32),
                pltpu.VMEM((6, *flat), jnp.float32),
                pltpu.VMEM((fields, span * cols, wide), jnp.float32),
                dma((peers,)),
                dma((peers,)),
                dma((STEPS, 4)),
                dma((STEPS, 4)),
                dma((peers, 2)),
                dma((peers, 2)),
                dma((3,)),
            ],
            compiler_params=pltpu.CompilerParams(
                collective_id=0, has_side_effects=True, vmem_limit_bytes=56 << 20
            ),
        )(
            solute.reshape(own, *flat),
            thermal.reshape(flat),
            eastward.reshape(flat),
            northward.reshape(flat),
            layers,
            rates,
            yields.reshape(1, tracers),
        )
        return mixture.reshape(solute.shape), heat.reshape(thermal.shape)

    return jax.shard_map(
        body,
        mesh=mesh,
        in_specs=(
            P("tracer", "region", "sect", None),
            P("region", "sect", None),
            P("region", "sect", None),
            P("region", "sect", None),
            P("region", "sect"),
            P(),
            P(),
        ),
        out_specs=(P("tracer", "region", "sect", None), P("region", "sect", None)),
        check_vma=False,
    )
```

```python
import functools

import jax
import jax.numpy as jnp
from jax import lax
from jax.experimental import pallas as pl
from jax.experimental.pallas import tpu as pltpu
from jax.sharding import PartitionSpec as P

STEPS = 3
SUB = 4

TIME_STEP = 0.2
REACT_STEP = 0.1
GROWTH_MAX = 1.0
HALF_SAT = 0.5
WATER_ATT = 3.0
CHL_ATT = 2.0
HEAT_GAIN = 0.5

MESH = pl.DeviceIdType.MESH
HIGHEST = lax.Precision.HIGHEST
EAST, WEST, NORTH, SOUTH = range(4)


def iota(shape, dim):
    return lax.broadcasted_iota(jnp.int32, shape, dim)


def exact_dot(a, b, dims=((1,), (0,))):
    return lax.dot_general(
        a, b, (dims, ((), ())), precision=HIGHEST, preferred_element_type=jnp.float32
    )


def halves(x):
    high = x.astype(jnp.bfloat16)
    return high, (x - high.astype(jnp.float32)).astype(jnp.bfloat16)


def half_dot(a, b):
    return jnp.dot(a, b, preferred_element_type=jnp.float32)


def dot3(a, b):
    return half_dot(a[0], b[0]) + half_dot(a[1], b[0]) + half_dot(a[0], b[1])


def tables(rates_ref, yields_ref, tracers, wide, Y):
    rows = tracers * Y
    spread = (iota((rows, tracers), 0) // Y == iota((rows, tracers), 1)).astype(jnp.float32)
    same = iota((rows, rows), 0) % Y == iota((rows, rows), 1) % Y
    full = exact_dot(exact_dot(spread, rates_ref[...]), spread, ((1,), (1,)))
    full = jnp.where(same, full, 0.0) * REACT_STEP
    diagonal = (iota((rows, rows), 0) == iota((rows, rows), 1)).astype(jnp.float32)
    one = diagonal + full
    two = exact_dot(one, one)
    three = exact_dot(two, one)
    four = exact_dot(two, two)
    source = [
        exact_dot(spread * yields_ref[...], jnp.ones((tracers, wide), jnp.float32)) * REACT_STEP
    ]
    for power in (one, two, three):
        source.append(exact_dot(power, source[0]))
    head = jnp.concatenate([power[: 3 * Y] for power in (one, two, three)], axis=0)
    shape = (rows, wide)
    lane = iota(shape, 1)
    inject = jnp.zeros(shape, jnp.float32)
    for sub in range(SUB):
        hit = jnp.logical_and(lane // Y == sub, lane % Y == iota(shape, 0) % Y)
        inject = inject + jnp.where(hit, source[SUB - 1 - sub], 0.0)
    return head, four, inject[:, : SUB * Y], [v[: 3 * Y] for v in source[: SUB - 1]]


def stack(flat, wide):
    return jnp.concatenate(
        [flat[:, i * wide : (i + 1) * wide] for i in range(flat.shape[1] // wide)], axis=0
    )


def unstack(tall, Y):
    return jnp.concatenate(
        [tall[i * Y : (i + 1) * Y] for i in range(tall.shape[0] // Y)], axis=1
    )


def plan(span):
    return (3, (0, 2, 1)) if span % 3 == 0 else (1, (0,))


def kernel(
    regions, groups, sects,
    solute, heat_hbm, east_hbm, north_hbm, layers_hbm, rates_hbm, yields_hbm,
    tracers_out, heat_out,
    layers_in, rates_ref, yields_ref,
    state, ysend, yrecv, coef, final,
    in_send, in_recv, halo_send, halo_recv, out_send, out_recv, local_sem, load_sem,
):
    region, group, sect = (lax.axis_index(a) for a in ("region", "tracer", "sect"))
    own, wide, Y = solute.shape[0], solute.shape[2], layers_in.shape[0]
    tracers = own * groups
    block = heat_hbm.shape[0] // groups
    span = block // Y
    fields = tracers + 1
    every = fields + 3

    def place(reg, t):
        return t + (reg % 2) * (groups - 1 - 2 * t)

    part = place(region, group)
    last = groups - 1
    next_region = lax.rem(region + 1, regions)
    past_region = lax.rem(region + regions - 1, regions)
    east_region = jnp.where(part == last, next_region, region)
    west_region = jnp.where(part == 0, past_region, region)
    east_part = jnp.where(part == last, 0, part + 1)
    west_part = jnp.where(part == 0, last, part - 1)
    beside = {
        EAST: {"region": east_region, "tracer": place(east_region, east_part)},
        WEST: {"region": west_region, "tracer": place(west_region, west_part)},
        NORTH: {"sect": lax.rem(sect + 1, sects)},
        SOUTH: {"sect": lax.rem(sect + sects - 1, sects)},
    }
    peers = [lax.rem(group + d, groups) for d in range(1, groups)]

    def rows_of(t):
        return pl.ds(pl.multiple_of(place(region, t) * block, Y), block)

    mine = rows_of(group)
    slot = pl.ds(group * own, own)
    inner = pl.ds(Y, block)

    barrier = pltpu.get_barrier_semaphore()
    for peer in peers:
        pl.semaphore_signal(barrier, inc=1, device_id={"tracer": peer}, device_id_type=MESH)
    for side in range(4):
        pl.semaphore_signal(barrier, inc=1, device_id=beside[side], device_id_type=MESH)
    keep = pltpu.make_async_copy(
        solute.at[:, mine, :], state.at[0, slot, inner, :], local_sem.at[0, 0]
    )
    keep.start()
    loads = []
    for i, (source_ref, target_ref) in enumerate(
        (
            (layers_hbm, layers_in),
            (rates_hbm, rates_ref),
            (yields_hbm, yields_ref),
            (heat_hbm.at[mine, :], state.at[0, tracers, inner, :]),
            (east_hbm.at[mine, :], state.at[0, fields, inner, :]),
            (north_hbm.at[mine, :], state.at[0, fields + 1, inner, :]),
        )
    ):
        copy = pltpu.make_async_copy(source_ref, target_ref, load_sem.at[i])
        copy.start()
        loads.append(copy)
    pl.semaphore_wait(barrier, groups - 1 + 4)

    chunks, order = plan(span)
    deep = span // chunks
    piece = deep * Y

    def part_of(t, c):
        return pl.ds(pl.multiple_of(place(region, t) * block + c * piece, Y), piece)

    arriving = {}
    for i, c in enumerate(order):
        for d, peer in enumerate(peers):
            copy = pltpu.make_async_remote_copy(
                src_ref=solute.at[:, part_of(peer, c), :],
                dst_ref=state.at[0, slot, pl.ds(Y + c * piece, piece), :],
                send_sem=in_send.at[d, c],
                recv_sem=in_recv.at[d, c],
                device_id={"tracer": peer},
                device_id_type=MESH,
            )
            copy.start()
            arriving[c, d] = copy

    for copy in loads:
        copy.wait()
    total = layers_in.shape[1] * Y
    pick = (iota((total, layers_in.shape[1]), 0) // Y == iota((total, layers_in.shape[1]), 1))
    depth = lax.dot_general(
        pick.astype(jnp.bfloat16),
        layers_in[...].astype(jnp.float32).astype(jnp.bfloat16),
        (((1,), (1,)), ((), ())),
        preferred_element_type=jnp.float32,
    )
    depth = jnp.where(iota((total, Y), 0) % Y == iota((total, Y), 1), depth, 0.0)
    depth = half_dot(depth.astype(jnp.bfloat16), jnp.ones((Y, wide), jnp.bfloat16))
    coef[5] = (iota((total, wide), 1).astype(jnp.float32) < depth).astype(jnp.float32)
    state[0, fields + 2, inner, :] = coef[5, mine, :]

    head, four, inject, source = tables(rates_ref, yields_ref, tracers, wide, Y)
    head, four, inject = halves(head), halves(four), halves(inject)
    upper = (iota((wide, wide), 0) < iota((wide, wide), 1)).astype(jnp.bfloat16)
    level = iota((piece, wide), 1).astype(jnp.float32) + 0.5
    tile = (1, deep)
    source = [jnp.tile(v, tile) for v in source]

    def light(chl_abs):
        high, low = halves(chl_abs)
        above = half_dot(high, upper) + half_dot(low, upper)
        return jnp.exp(
            -(WATER_ATT / wide * level + CHL_ATT / wide * (above + 0.5 * chl_abs))
        )

    sent = []

    def exchange(step, c):
        count = every if step == 0 else fields
        some = pl.ds(0, count)
        moves = {}
        if c == chunks - 1:
            moves[EAST] = (
                state.at[step, some, pl.ds(block, Y), :],
                state.at[step, some, pl.ds(0, Y), :],
            )
        if c == 0:
            moves[WEST] = (
                state.at[step, some, pl.ds(Y, Y), :],
                state.at[step, some, pl.ds(block + Y, Y), :],
            )

        def send(moves):
            for side, (source_ref, target_ref) in moves.items():
                copy = pltpu.make_async_remote_copy(
                    src_ref=source_ref,
                    dst_ref=target_ref,
                    send_sem=halo_send.at[step, c, side],
                    recv_sem=halo_recv.at[step, c, side],
                    device_id=beside[side],
                    device_id_type=MESH,
                )
                copy.start()
                sent.append(copy)
                halos[step, c, side] = copy

        send(moves)
        for f in range(count):
            for side, y in ((0, 0), (1, Y - 1)):
                ysend[step, c, side, f] = state[
                    step, f, pl.ds(Y + c * piece + y, deep, stride=Y), :
                ]
        moves = {
            NORTH: (ysend.at[step, c, 1, some], yrecv.at[step, c, 1, some]),
            SOUTH: (ysend.at[step, c, 0, some], yrecv.at[step, c, 0, some]),
        }
        send(moves)

    halos = {}

    def beside_y(step, value, x, first, count):
        at = (count, Y, wide)
        row = iota(at, 1)
        some = pl.ds(first, count)
        above = jnp.broadcast_to(yrecv[step, x // deep, 0, some, pl.ds(x % deep, 1), :], at)
        below = jnp.broadcast_to(yrecv[step, x // deep, 1, some, pl.ds(x % deep, 1), :], at)
        up = jnp.where(row == Y - 1, above, pltpu.roll(value, Y - 1, 1))
        down = jnp.where(row == 0, below, pltpu.roll(value, 1, 1))
        return up, down

    keep.wait()
    for c in order:
        for d in range(len(peers)):
            arriving[c, d].wait_recv()
        exchange(0, c)

    leaving = []

    def leave(c):
        rows = pl.ds(c * piece, piece)
        out_rows = part_of(group, c)
        for d, peer in enumerate(peers):
            pairs = (
                (final.at[pl.ds(peer * own, own), rows, :], tracers_out.at[:, out_rows, :]),
                (final.at[tracers, rows, :], heat_out.at[out_rows, :]),
            )
            for i, (source_ref, target_ref) in enumerate(pairs):
                copy = pltpu.make_async_remote_copy(
                    src_ref=source_ref,
                    dst_ref=target_ref,
                    send_sem=out_send.at[d, c, i],
                    recv_sem=out_recv.at[d, c, i],
                    device_id={"tracer": peer},
                    device_id_type=MESH,
                )
                copy.start()
                leaving.append(copy)
        pairs = (
            (final.at[slot, rows, :], tracers_out.at[:, out_rows, :]),
            (final.at[tracers, rows, :], heat_out.at[out_rows, :]),
        )
        for i, (source_ref, target_ref) in enumerate(pairs):
            copy = pltpu.make_async_copy(source_ref, target_ref, local_sem.at[c, 1 + i])
            copy.start()
            leaving.append(copy)

    def advance(step, c):
        columns, heats, wets = [], [], []
        for x in range(c * deep, (c + 1) * deep):
            here = pl.ds((x + 1) * Y, Y)
            ahead = pl.ds((x + 2) * Y, Y)
            behind = pl.ds(x * Y, Y)
            cell = pl.ds(x * Y, Y)
            if step == 0:
                speed_wet = state[0, pl.ds(fields + 1, 2), here, :]
                up, down = beside_y(0, speed_wet, x, fields + 1, 2)
                wet = speed_wet[1]
                east = state[0, fields, here, :] * wet * state[0, fields + 2, ahead, :]
                west = state[0, fields, behind, :] * state[0, fields + 2, behind, :] * wet
                north = speed_wet[0] * wet * up[1]
                south = down[0] * down[1] * wet
                scaled = TIME_STEP * wet
                coef[0, cell, :] = wet - scaled * (
                    jnp.maximum(east, 0.0) - jnp.minimum(west, 0.0)
                    + jnp.maximum(north, 0.0) - jnp.minimum(south, 0.0)
                )
                coef[1, cell, :] = -scaled * jnp.minimum(east, 0.0)
                coef[2, cell, :] = scaled * jnp.maximum(west, 0.0)
                coef[3, cell, :] = -scaled * jnp.minimum(north, 0.0)
                coef[4, cell, :] = scaled * jnp.maximum(south, 0.0)
            value = state[step, pl.ds(0, fields), here, :]
            up, down = beside_y(step, value, x, 0, fields)
            moved = (
                coef[0, cell, :] * value
                + coef[1, cell, :] * state[step, pl.ds(0, fields), ahead, :]
                + coef[2, cell, :] * state[step, pl.ds(0, fields), behind, :]
                + coef[3, cell, :] * up
                + coef[4, cell, :] * down
            )
            columns.append(moved[:tracers].reshape(tracers * Y, wide))
            heats.append(moved[tracers])
            wets.append(state[0, fields + 2, here, :])
        mixed = jnp.concatenate(columns, axis=1)
        parts = halves(mixed)
        ahead_rows = dot3(head, parts)
        result = dot3(four, parts)
        rates = []
        for sub in range(SUB):
            if sub == 0:
                rows = mixed[: 3 * Y]
            else:
                rows = ahead_rows[(sub - 1) * 3 * Y : sub * 3 * Y]
                for i, rate in enumerate(rates):
                    rows = rows + source[sub - 1 - i] * jnp.concatenate([rate] * 3, axis=0)
            nutrient, chl, phyto = rows[:Y], rows[Y : 2 * Y], rows[2 * Y :]
            shade = unstack(light(jnp.abs(stack(chl, wide))), Y)
            rates.append(
                GROWTH_MAX * shade * nutrient / (jnp.abs(nutrient) + HALF_SAT) * phyto
            )
        result = result + dot3(inject, halves(jnp.concatenate(rates, axis=0)))
        chl_abs = jnp.abs(stack(result[Y : 2 * Y], wide))
        heating = HEAT_GAIN * chl_abs * light(chl_abs)
        heat = jnp.concatenate(heats, axis=0) + TIME_STEP * jnp.concatenate(wets, axis=0) * heating
        if step < STEPS - 1:
            target, base = state.at[step + 1], Y + c * piece
        else:
            target, base = final, c * piece
        for x in range(deep):
            target[pl.ds(0, tracers), pl.ds(base + x * Y, Y), :] = result[
                :, x * wide : (x + 1) * wide
            ].reshape(tracers, Y, wide)
        target[tracers, pl.ds(base, piece), :] = heat

    for step in range(STEPS):
        for c in order:
            for side in (NORTH, SOUTH):
                halos[step, c, side].wait_recv()
            if c == 0:
                halos[step, chunks - 1, EAST].wait_recv()
            if c == chunks - 1:
                halos[step, 0, WEST].wait_recv()
            advance(step, c)
            if step < STEPS - 1:
                exchange(step + 1, c)
            else:
                leave(c)
    for copy in leaving:
        copy.wait()
    for copy in sent + list(arriving.values()):
        copy.wait_send()


def solution(mesh):
    regions, groups, sects = (mesh.shape[a] for a in ("region", "tracer", "sect"))

    def body(solute, thermal, eastward, northward, layers, rates, yields):
        own, rows, cols, wide = solute.shape
        tracers = own * groups
        span = rows // groups
        fields = tracers + 1
        flat = (rows * cols, wide)
        free, hbm = pl.BlockSpec(memory_space=pl.ANY), pl.BlockSpec(memory_space=pltpu.HBM)
        dma = pltpu.SemaphoreType.DMA
        peers = max(groups - 1, 1)
        chunks = plan(span)[0]
        mixture, heat = pl.pallas_call(
            functools.partial(kernel, regions, groups, sects),
            out_shape=(
                jax.ShapeDtypeStruct((own, *flat), jnp.float32),
                jax.ShapeDtypeStruct(flat, jnp.float32),
            ),
            in_specs=[hbm] * 7,
            out_specs=(free, free),
            scratch_shapes=[
                pltpu.VMEM((cols, rows), jnp.int32),
                pltpu.VMEM((tracers, tracers), jnp.float32),
                pltpu.VMEM((1, tracers), jnp.float32),
                pltpu.VMEM((STEPS, fields + 3, (span + 2) * cols, wide), jnp.float32),
                pltpu.VMEM((STEPS, chunks, 2, fields + 3, span // chunks, wide), jnp.float32),
                pltpu.VMEM((STEPS, chunks, 2, fields + 3, span // chunks, wide), jnp.float32),
                pltpu.VMEM((6, *flat), jnp.float32),
                pltpu.VMEM((fields, span * cols, wide), jnp.float32),
                dma((peers, chunks)),
                dma((peers, chunks)),
                dma((STEPS, chunks, 4)),
                dma((STEPS, chunks, 4)),
                dma((peers, chunks, 2)),
                dma((peers, chunks, 2)),
                dma((chunks, 3)),
                dma((6,)),
            ],
            compiler_params=pltpu.CompilerParams(
                collective_id=0, has_side_effects=True, vmem_limit_bytes=60 << 20
            ),
        )(
            solute.reshape(own, *flat),
            thermal.reshape(flat),
            eastward.reshape(flat),
            northward.reshape(flat),
            layers.T,
            rates,
            yields.reshape(1, tracers),
        )
        return mixture.reshape(solute.shape), heat.reshape(thermal.shape)

    return jax.shard_map(
        body,
        mesh=mesh,
        in_specs=(
            P("tracer", "region", "sect", None),
            P("region", "sect", None),
            P("region", "sect", None),
            P("region", "sect", None),
            P("region", "sect"),
            P(),
            P(),
        ),
        out_specs=(P("tracer", "region", "sect", None), P("region", "sect", None)),
        check_vma=False,
    )
```
